512 devices in a mesh: rack: 32 (over x, y), expert: 16 (over z, core).
Axes of the slice: x: 4, y: 8, z: 8, core: 2. Of those that a mesh axis runs over, the one named last changes fastest.
Arguments:
- hidden_in: bfloat16 [512, 3584], P(('rack', 'expert')), may hold values from -6 to 6
- norm_gain: float32 [3584], replicated, may hold values from 0.1 to 1.9
- expert_ids: int32 [4, 512, 8], P(None, ('rack', 'expert')), may hold values from 0 to 31, all different within a row; in each aligned block of 16 rows (0 to 15, 16 to 31, ..., all dimensions but the last counted through in order) at most 6 rows name the same one
- gate_levels: int32 [4, 512, 8], P(None, ('rack', 'expert')), may hold values from 1 to 255
- w_gate_up: bfloat16 [32, 16, 1792, 2, 256], P('rack', 'expert'), may hold values from -0.09375 to 0.09375
- w_down: bfloat16 [32, 16, 256, 1792], P('rack', 'expert'), may hold values from -0.125 to 0.125
Outputs:
- hidden_out: float32 [512, 3584], P(('rack', 'expert'))
The draws below stay inside these ranges and needn't reach their ends.
Inputs may be any that keep to these rules, and one draw needn't show every extreme that they name: `expert_ids`: each token names 8 different experts in each step; in each step at most 6 of the 16 tokens of one index of rack (an aligned block of the token order) name the same expert, and that many do in some blocks.
All inputs are finite; a program needn't handle non-finite values.
Results may differ from the reference program's by a relative error of at most 0.015.
Values may be sent and summed in bfloat16 or wider, within the bound.
A program may use at most 64 MiB of HBM per device.

```python
import math
import jax
import jax.numpy as jnp
import numpy as np
from jax import lax

D = 3584
HID = 2048
TOP = 8
STEPS = 4
TOK_DEV = 1
EXPERTS = 32
HPART = 256
RACK_ROWS = 16
TOKENS = 512
CAP = 6
N_RACK = 32
N_EXPERT = 16


def touch_ends(entries, key, smallest, high):
    longest = entries.shape.index(max(entries.shape))
    spots = []
    for shift in (0, 1):
        where = [jax.random.randint(jax.random.fold_in(key, axis), (), 0, length) for axis, length in enumerate(entries.shape)]
        where[longest] = (where[longest] + shift) % entries.shape[longest]
        spots.append(tuple(where))
    return entries.at[spots[0]].set(smallest).at[spots[1]].set(high)


def block_levels(own_key, shape, split, least, largest):
    def one(axis_at, parts):
        steps = jax.random.uniform(jax.random.fold_in(jax.random.fold_in(own_key, 6), axis_at), (parts,), jnp.float32, least / len(split), largest / len(split))
        return jnp.repeat(jnp.exp(steps), shape[axis_at] // parts).reshape((-1,) + (1,) * (len(shape) - axis_at - 1))

    loudness = one(*split[0])
    for cut in split[1:]:
        loudness = loudness * one(*cut)
    return loudness


def routed_block(own_key, own, number, rows, number_of, top, most, skew):
    ranking = jax.random.permutation(own_key, number_of)
    crowded, ordinary = portions_of(number_of, rows * top, most, skew, True), portions_of(number_of, rows * top, most, skew, False)
    places = jnp.arange(number_of)

    def named(tallies, rotation):
        used = int((tallies > 0).sum())
        fixed = max(1, used // 4)
        moved = fixed + (places - fixed + rotation * (used - fixed)) % max(1, number_of - fixed)
        return jnp.zeros((number_of,), jnp.int32).at[ranking[jnp.where(places < fixed, places, moved)]].set(jnp.asarray(tallies, jnp.int32))

    tallies = jnp.where(number % 4 == 0, named(crowded, number // 4), named(ordinary, number - number // 4 - 1))
    mixed = jax.random.permutation(jax.random.fold_in(own, 3), number_of)
    donor, taker = mixed[0:number_of // 2 * 2:2], mixed[1:number_of // 2 * 2:2]
    room = jnp.minimum(tallies[donor] - 1, most - tallies[taker]) // 2
    room = jnp.where((donor == ranking[0]) | (taker == ranking[0]) | (tallies[taker] == 0), 0, jnp.maximum(room, 0))
    moved = jax.random.randint(jax.random.fold_in(own, 4), (number_of // 2,), 0, 1 << 20) % (room + 1)
    tallies = tallies.at[donor].add(-moved).at[taker].add(moved)
    items = jnp.searchsorted(jnp.cumsum(tallies), jnp.arange(rows * top), side="right").astype(jnp.int32)
    grid = items.reshape(top, rows).T
    grid = grid[jax.random.permutation(jax.random.fold_in(own, 1), rows)]
    rotation = jax.random.randint(jax.random.fold_in(own, 2), (rows, 1), 0, top)
    return jnp.take_along_axis(grid, (jnp.arange(top)[None, :] + rotation) % top, axis=1)


def portions_of(count, total, most, lean, full):
    loads = [(1 << 20) // math.isqrt(rank ** lean) + 1 for rank in range(1, count + 1)]
    largest = most if full else min(most, max(-(-total // count), total * loads[0] // sum(loads)))
    least = 1 if total - largest >= count - 1 else 0
    counts, spare = [largest] + [least] * (count - 1), total - largest - least * (count - 1)
    while spare > 0:
        movable = [i for i in range(1, count) if counts[i] < largest] or [i for i in range(1, count) if counts[i] < most]
        mass, left = sum([loads[i] for i in movable]), spare
        for i in movable:
            extra = min(most - counts[i], max(1, left * loads[i] // mass), spare)
            counts[i] = counts[i] + extra
            spare = spare - extra
    return np.array(counts)


def normal_values(key, shape, width, reach, pieces=(), kind=jnp.bfloat16):
    factor_of = block_levels(key, shape, pieces, -0.22, 0.18) if pieces else 1.0
    array = jax.random.normal(key, shape, jnp.float32) * width * factor_of
    return jnp.minimum(jnp.maximum(array, -reach), reach).astype(kind)


def setup_inputs(seed: int = 0) -> dict:
    streams_of = jax.random.split(jax.random.key(seed), 7)
    hidden_in = normal_values(streams_of[0], (TOKENS, D), 1.0, 6.0, ((0, 512),))
    norm_gain = jnp.clip(1.0 + 0.18 * jax.random.normal(streams_of[1], (D,), jnp.float32), 0.1, 1.9)
    expert_ids_keys = jax.random.split(jax.random.fold_in(streams_of[2], 1), STEPS * TOKENS // RACK_ROWS)
    expert_ids_turns = jax.random.permutation(jax.random.fold_in(streams_of[2], 3), STEPS * TOKENS // RACK_ROWS)
    expert_ids = jax.vmap(lambda own, number: routed_block(jax.random.fold_in(streams_of[2], 2), own, number, RACK_ROWS, EXPERTS, TOP, CAP, 2))(expert_ids_keys, expert_ids_turns).reshape((STEPS, TOKENS, TOP))
    gate_levels = touch_ends(jax.random.randint(streams_of[3], (STEPS, TOKENS, TOP), 1, 256), jax.random.fold_in(streams_of[3], 1), 1, 255).astype(jnp.int32)
    w_gate_up = normal_values(streams_of[4], (EXPERTS, N_EXPERT, D // 2, 2, HPART), D ** -0.5, 0.09375, ((0, 32), (1, 16)))
    w_down = normal_values(streams_of[5], (EXPERTS, N_EXPERT, HPART, D // 2), HID ** -0.5, 0.125, ((0, 32), (1, 16)))
    return {"hidden_in": hidden_in, "norm_gain": norm_gain, "expert_ids": expert_ids, "gate_levels": gate_levels, "w_gate_up": w_gate_up, "w_down": w_down}


def reference(hidden_in, norm_gain, expert_ids, gate_levels, w_gate_up, w_down):
    residual = hidden_in.astype(jnp.float32)
    rack_rows = TOK_DEV * N_EXPERT
    group_total = N_EXPERT // 2
    half_width = D // 2
    token_ids = jnp.arange(TOKENS, dtype=jnp.int32).reshape(N_RACK, rack_rows)
    slot_ids = jnp.arange(CAP, dtype=jnp.int32)
    expert_range = jnp.arange(EXPERTS, dtype=jnp.int32)
    for step_index in range(STEPS):
        mean_square = lax.optimization_barrier(jnp.mean(residual * residual, axis=-1, keepdims=True))
        normed = (residual * lax.rsqrt(mean_square + 1e-06) * norm_gain).astype(jnp.bfloat16)
        picked = expert_ids[step_index]
        level_vals = gate_levels[step_index].astype(jnp.float32)
        shares = level_vals / lax.optimization_barrier(jnp.sum(level_vals, axis=-1, keepdims=True))
        matches = picked[:, :, None] == expert_range[None, None, :]
        chosen = lax.optimization_barrier(jnp.sum(matches.astype(jnp.int32), axis=1))
        mixing = lax.optimization_barrier(jnp.sum(jnp.where(matches, shares[:, :, None], jnp.float32(0.0)), axis=1)).astype(jnp.bfloat16)
        mixing = lax.optimization_barrier(mixing).astype(jnp.float32)
        per_rack = chosen.reshape(N_RACK, rack_rows, EXPERTS)
        slot_rank = jnp.cumsum(per_rack, axis=1) - per_rack
        placement = per_rack[..., None] * (slot_rank[..., None] == slot_ids).astype(jnp.int32)
        token_index = lax.optimization_barrier(jnp.sum(placement * token_ids[:, :, None, None], axis=1))
        valid_rows = lax.optimization_barrier(jnp.sum(placement, axis=1))
        token_index = jnp.transpose(token_index, (1, 0, 2)).reshape(EXPERTS, N_RACK * CAP).astype(jnp.int32)
        valid_rows = jnp.transpose(valid_rows, (1, 0, 2)).reshape(EXPERTS, N_RACK * CAP)

        def expert_term(packed):
            expert_id, row_index, row_valid = packed
            slot_rows = normed[row_index] * row_valid[:, None].astype(jnp.bfloat16)
            gate_up_parts = w_gate_up[expert_id].reshape(group_total, 2, half_width, 2, HPART)
            gate_up_full = jnp.transpose(gate_up_parts, (1, 2, 3, 0, 4)).reshape(D, 2 * HID)
            gate_up = jnp.dot(slot_rows, gate_up_full, preferred_element_type=jnp.float32)
            activated = (jax.nn.silu(gate_up[:, :HID]) * gate_up[:, HID:]).astype(jnp.bfloat16)
            down_parts = w_down[expert_id].reshape(group_total, 2, HPART, half_width)
            down_full = jnp.transpose(down_parts, (0, 2, 1, 3)).reshape(group_total, HPART, D)
            partial_value = jnp.einsum('ngh,ghd->ngd', activated.reshape(-1, group_total, HPART).astype(jnp.float32), down_full.astype(jnp.float32))
            rounded = lax.optimization_barrier(partial_value.astype(jnp.bfloat16))
            return lax.optimization_barrier(jnp.sum(rounded.astype(jnp.float32), axis=1))
        outputs = lax.map(expert_term, (expert_range, token_index, valid_rows))
        slot_weight = mixing[token_index, expert_range[:, None]] * valid_rows.astype(jnp.float32)
        update = jax.ops.segment_sum((outputs * slot_weight[:, :, None]).reshape(-1, D), token_index.reshape(-1), num_segments=TOKENS)
        residual = residual + update
    return residual
```

```python
import functools

import jax
import jax.numpy as jnp
from jax import lax
from jax.experimental import pallas as pl
from jax.experimental.pallas import tpu as pltpu
from jax.sharding import PartitionSpec as P

MESH = pl.DeviceIdType.MESH
BF16 = jnp.bfloat16
F32 = jnp.float32
TILE = 128
GRID = (4, 8, 8)
ORDERS = (("y", "x", "z"), ("y", "z", "x"), ("z", "x", "y"))
STORED = ("z", "y", "x")


def shares_of(tiles):
    first = (tiles + 1) // 3
    second = (tiles + 1 - first) // 2
    return (first - 1, second, tiles + 1 - first - second)


def kernel(
    grid, steps, top, experts, widths,
    hid_ref, gain_ref, ids_ref, lev_ref, wgu_ref, wd_ref, out_ref,
    ga, gb, gc, pa, pb, pc, gu_ref, act_ref, xs_ref, xr_ref,
    res_ref, mix_ref, mixs_ref, mixr_ref, hs_ref, hr_ref, fs_ref, fr_ref, sss_ref, ssr_ref,
    rr_a, rr_b, rr_c, st_a, st_b, st_c, u_a, u_b, u_c, v_a, v_b, v_c, w_a, w_b, w_c, t_a, t_b, t_c,
    ag_send, ag_recv, rs_send, rs_recv, pair_send, pair_recv,
):
    size = dict(zip("xyz", grid))
    rack, col = lax.axis_index("rack"), lax.axis_index("expert")
    here = {"x": rack // size["y"], "y": rack % size["y"], "z": col // 2}
    core = col % 2
    half = sum(widths)
    tokens = 2 * grid[0] * grid[1] * grid[2]
    starts = (0, widths[0], widths[0] + widths[1])
    gathered, partial = (ga, gb, gc), (pa, pb, pc)
    ring_in, ring_out = (rr_a, rr_b, rr_c), (st_a, st_b, st_c)
    mid_out, mid_in = (u_a, u_b, u_c), (v_a, v_b, v_c)
    last_out, last_in = (w_a, w_b, w_c), (t_a, t_b, t_c)

    def device(at):
        return (at["x"] * size["y"] + at["y"], at["z"] * 2 + core)

    def away(axis, shift):
        n = size[axis]
        return lax.rem(here[axis] + (shift + n) % n, n)

    def moved(axis, shift):
        return device({**here, axis: away(axis, shift)})

    mate = (rack, col + 1 - 2 * core)

    def where_at(full, axis=None, at=None):
        return tuple(
            pl.ds(0, size[a]) if a in full else (at if a == axis else here[a]) for a in STORED
        )

    def to_mate(src, dst, slot):
        return pltpu.make_async_remote_copy(
            src_ref=src, dst_ref=dst, send_sem=pair_send.at[slot], recv_sem=pair_recv.at[slot],
            device_id=mate, device_id_type=MESH,
        )

    barrier = pltpu.get_barrier_semaphore()
    partners = [mate] + [moved(a, d) for a in "xyz" for d in range(1, size[a])]
    for partner in partners:
        pl.semaphore_signal(barrier, inc=1, device_id=partner, device_id_type=MESH)

    own = hid_ref[...].astype(F32)
    low, high = own[:, :half], own[:, half:]
    first_core = core == 0
    hs_ref[...] = jnp.where(first_core, high, low)
    levels = lev_ref[...].astype(F32)
    shares = levels / jnp.sum(levels, axis=-1, keepdims=True)
    chosen = ids_ref[...]
    lanes = lax.broadcasted_iota(jnp.int32, (steps, TILE), 1)
    mixing = jnp.zeros((steps, TILE), F32)
    for k in range(top):
        mixing += jnp.where(lanes == chosen[:, k : k + 1], shares[:, k : k + 1], 0.0)
    mixs_ref[...] = mixing
    pl.semaphore_wait(barrier, len(partners))
    sent = [to_mate(hs_ref, hr_ref, 0), to_mate(mixs_ref, mixr_ref, 1)]
    for copy in sent:
        copy.start()
    for copy in sent:
        copy.wait()
    row = lax.broadcasted_iota(jnp.int32, (2, half), 0)
    res_ref[...] = jnp.where(row == core, jnp.where(first_core, low, high), hr_ref[...])
    mix_row = lax.broadcasted_iota(jnp.int32, (2, TILE), 0)
    for s in range(steps):
        mix_ref[s] = jnp.where(mix_row == core, mixing[s : s + 1], mixr_ref[s : s + 1, :])
    gains = gain_ref[...]
    gain = jnp.where(first_core, gains[:, :half], gains[:, half:])

    def ag_copy(o, phase, slot, axis, full, at, shift):
        ref = gathered[o].at[where_at(full, axis, at)]
        return pltpu.make_async_remote_copy(
            src_ref=ref, dst_ref=ref, send_sem=ag_send.at[o, phase, slot],
            recv_sem=ag_recv.at[o, phase, slot], device_id=moved(axis, shift), device_id_type=MESH,
        )

    def rs_copy(o, phase, slot, src, dst, axis, shift):
        return pltpu.make_async_remote_copy(
            src_ref=src, dst_ref=dst, send_sem=rs_send.at[o, phase, slot],
            recv_sem=rs_recv.at[o, phase, slot], device_id=moved(axis, shift), device_id_type=MESH,
        )

    def ring_counts(axis):
        n = size[axis]
        return n // 2, n - 1 - n // 2

    def one_step(step, carry):
        residual = res_ref[...]
        sss_ref[...] = jnp.broadcast_to(
            jnp.sum(residual * residual, axis=-1, keepdims=True), sss_ref.shape
        )
        copy = to_mate(sss_ref, ssr_ref, 2)
        copy.start()
        copy.wait()
        total = (sss_ref[...] + ssr_ref[...])[:, :1]
        normed = (residual * lax.rsqrt(total / (2 * half) + 1e-6) * gain).astype(BF16)
        for o in range(3):
            block = normed[:, starts[o] : starts[o] + widths[o]]
            if o == 0:
                block = jnp.concatenate([block, mix_ref[step].astype(BF16)], axis=1)
            gathered[o][where_at(())] = block

        sends = []
        for phase in range(2):
            flying = []
            for o in range(3):
                if phase:
                    for copy in waits[o]:
                        copy.wait_recv()
                axis, full = ORDERS[o][phase], ORDERS[o][:phase]
                flying.append([
                    ag_copy(o, phase, d - 1, axis, full, here[axis], d)
                    for d in sorted(range(1, size[axis]), key=lambda d: -min(d, size[axis] - d))
                ])
                for copy in flying[o]:
                    copy.start()
                sends += flying[o]
            waits = flying
        rounds = max(size[o[2]] // 2 for o in ORDERS)
        for t in range(1, rounds + 1):
            flying = []
            for o in range(3):
                for copy in waits[o]:
                    copy.wait_recv()
                axis, full = ORDERS[o][2], ORDERS[o][:2]
                right, left = ring_counts(axis)
                copies = []
                if t <= right:
                    copies.append(ag_copy(o, 2, t - 1, axis, full, away(axis, 1 - t), 1))
                if t <= left:
                    copies.append(ag_copy(o, 2, right + t - 1, axis, full, away(axis, t - 1), -1))
                for copy in copies:
                    copy.start()
                sends += copies
                flying.append(copies)
            waits = flying
        for o in range(3):
            for copy in waits[o]:
                copy.wait_recv()

        chunk = tokens // size["z"]
        swaps = []
        for z in range(size["z"]):
            rows = pl.ds(z * chunk, chunk)
            total = None
            for o in range(3):
                x = gathered[o][z].reshape(chunk, gathered[o].shape[-1])[:, : widths[o]]
                part = jnp.dot(
                    x, wgu_ref[starts[o] : starts[o] + widths[o], :], preferred_element_type=F32
                )
                total = part if total is None else total + part
            gu_ref[rows, :] = total
            xs_ref[rows, :] = total.astype(BF16)
            swap = to_mate(xs_ref.at[rows], xr_ref.at[rows], 3 + z)
            swap.start()
            swaps.append(swap)
        hidden = wd_ref.shape[0]
        mine = (
            lax.broadcasted_iota(jnp.int32, (tokens, TILE), 1) == rack
        )
        weight = jnp.sum(
            jnp.where(mine, ga[..., widths[0] :].reshape(tokens, TILE).astype(F32), 0.0),
            axis=-1, keepdims=True,
        )
        for z in range(size["z"]):
            rows = pl.ds(z * chunk, chunk)
            swaps[z].wait()
            both = gu_ref[rows, :] + xr_ref[rows, :].astype(F32)
            gate, up = both[:, :hidden], both[:, hidden:]
            act_ref[rows, :] = (gate / (1.0 + jnp.exp(-gate)) * up).astype(BF16)
        for copy in sends:
            copy.wait_send()
        for o in range(3):
            part = jnp.dot(
                act_ref[...], wd_ref[:, starts[o] : starts[o] + widths[o]],
                preferred_element_type=F32,
            )
            partial[o][...] = (part * weight).astype(BF16).reshape(partial[o].shape)

        sends = []
        waits = [[], [], []]
        for t in range(1, rounds + 1):
            flying = []
            for o in range(3):
                axis, full = ORDERS[o][2], ORDERS[o][:2]
                right, left = ring_counts(axis)
                copies = []
                for count, base, sign in ((right, 0, 1), (left, right, -1)):
                    if t > count:
                        continue
                    slot = base + t - 1
                    at = where_at(full, axis, away(axis, sign * (count - t + 1)))
                    if t == 1:
                        src = partial[o].at[at]
                    else:
                        waits[o][0 if sign > 0 else 1].wait_recv()
                        ring_out[o][slot] = ring_in[o][slot - 1] + partial[o][at]
                        src = ring_out[o].at[slot]
                    copy = rs_copy(o, 0, slot, src, ring_in[o].at[slot], axis, sign)
                    copy.start()
                    copies.append(copy)
                sends += copies
                if waits[o] and len(copies) < len(waits[o]):
                    copies = copies + waits[o][len(copies):]
                flying.append(copies)
            waits = flying
        for o in range(3):
            axis, full = ORDERS[o][2], ORDERS[o][:2]
            right, left = ring_counts(axis)
            for copy in waits[o]:
                copy.wait_recv()
            total = partial[o][where_at(full, axis, here[axis])].astype(F32)
            total += ring_in[o][right - 1].astype(F32)
            if left:
                total += ring_in[o][right + left - 1].astype(F32)
            mid_out[o][...] = total.astype(BF16)

        flying = []
        for o in range(3):
            axis = ORDERS[o][1]
            other = [a for a in STORED if a in ORDERS[o][:2]]
            copies = []
            for d in range(1, size[axis]):
                at = tuple(
                    away(axis, d) if a == axis else pl.ds(0, size[a]) for a in other
                )
                copies.append(
                    rs_copy(o, 1, d - 1, mid_out[o].at[at], mid_in[o].at[d - 1], axis, d)
                )
            for copy in copies:
                copy.start()
            sends += copies
            flying.append(copies)
        waits = flying
        flying = []
        for o in range(3):
            axis = ORDERS[o][1]
            other = [a for a in STORED if a in ORDERS[o][:2]]
            at = tuple(here[axis] if a == axis else pl.ds(0, size[a]) for a in other)
            total = mid_out[o][at].astype(F32)
            for d in range(1, size[axis]):
                waits[o][d - 1].wait_recv()
                total += mid_in[o][d - 1].astype(F32)
            last_out[o][...] = total.astype(BF16)
            axis = ORDERS[o][0]
            copies = [
                rs_copy(o, 2, d - 1, last_out[o].at[away(axis, d)], last_in[o].at[d - 1], axis, d)
                for d in range(1, size[axis])
            ]
            for copy in copies:
                copy.start()
            sends += copies
            flying.append(copies)
        waits = flying
        for o in range(3):
            axis = ORDERS[o][0]
            total = last_out[o][here[axis]].astype(F32)
            for d in range(1, size[axis]):
                waits[o][d - 1].wait_recv()
                total += last_in[o][d - 1].astype(F32)
            res_ref[:, starts[o] : starts[o] + widths[o]] += total
        for copy in sends:
            copy.wait_send()
        return carry

    lax.fori_loop(0, steps, one_step, 0)

    residual = res_ref[...]
    fs_ref[...] = jnp.where(first_core, residual[1:2], residual[0:1])
    copy = to_mate(fs_ref, fr_ref, 2)
    copy.start()
    kept = jnp.where(first_core, residual[0:1], residual[1:2])
    copy.wait()
    out_ref[:, :half] = jnp.where(first_core, kept, fr_ref[...])
    out_ref[:, half:] = jnp.where(first_core, fr_ref[...], kept)


def per_device(grid, hidden_in, norm_gain, expert_ids, gate_levels, w_gate_up, w_down):
    steps, _, top = expert_ids.shape
    width = hidden_in.shape[1]
    half = width // 2
    hidden = w_down.shape[2]
    tokens = 2 * grid[0] * grid[1] * grid[2]
    widths = tuple(TILE * n for n in shares_of(half // TILE))
    size = dict(zip("xyz", grid))
    stored = tuple(size[a] for a in STORED)

    def dims(names):
        return tuple(size[a] for a in STORED if a in names)

    scratch = [pltpu.VMEM(stored + (2, w + (TILE if o == 0 else 0)), BF16) for o, w in enumerate(widths)]
    scratch += [pltpu.VMEM(stored + (2, w), BF16) for w in widths]
    scratch += [
        pltpu.VMEM((tokens, 2 * hidden), F32),
        pltpu.VMEM((tokens, hidden), BF16),
        pltpu.VMEM((tokens, 2 * hidden), BF16),
        pltpu.VMEM((tokens, 2 * hidden), BF16),
        pltpu.VMEM((2, half), F32),
        pltpu.VMEM((steps, 2, TILE), F32),
        pltpu.VMEM((steps, TILE), F32),
        pltpu.VMEM((steps, TILE), F32),
        pltpu.VMEM((1, half), F32),
        pltpu.VMEM((1, half), F32),
        pltpu.VMEM((1, half), F32),
        pltpu.VMEM((1, half), F32),
        pltpu.VMEM((2, TILE), F32),
        pltpu.VMEM((2, TILE), F32),
    ]
    for _ in range(2):
        scratch += [
            pltpu.VMEM((size[o[2]] - 1,) + dims(o[:2]) + (2, w), BF16) for o, w in zip(ORDERS, widths)
        ]
    scratch += [pltpu.VMEM(dims(o[:2]) + (2, w), BF16) for o, w in zip(ORDERS, widths)]
    scratch += [
        pltpu.VMEM((size[o[1]] - 1, size[o[0]], 2, w), BF16) for o, w in zip(ORDERS, widths)
    ]
    scratch += [pltpu.VMEM((size[o[0]], 2, w), BF16) for o, w in zip(ORDERS, widths)]
    scratch += [pltpu.VMEM((size[o[0]] - 1, 2, w), BF16) for o, w in zip(ORDERS, widths)]
    most = max(grid) - 1
    scratch += [pltpu.SemaphoreType.DMA((3, 3, most))] * 4
    scratch += [pltpu.SemaphoreType.DMA((3 + size["z"],))] * 2
    return pl.pallas_call(
        functools.partial(kernel, grid, steps, top, 0, widths),
        out_shape=jax.ShapeDtypeStruct((1, width), F32),
        in_specs=[pl.BlockSpec(memory_space=pltpu.VMEM)] * 6,
        out_specs=pl.BlockSpec(memory_space=pltpu.VMEM),
        scratch_shapes=scratch,
        compiler_params=pltpu.CompilerParams(
            collective_id=0, has_side_effects=True, vmem_limit_bytes=48 << 20
        ),
    )(
        hidden_in,
        norm_gain.reshape(1, width),
        expert_ids[:, 0, :],
        gate_levels[:, 0, :],
        w_gate_up[0, 0].reshape(half, 2 * hidden),
        w_down[0, 0],
    )


def solution(mesh, grid=GRID):
    in_specs = (
        P(("rack", "expert"), None),
        P(),
        P(None, ("rack", "expert"), None),
        P(None, ("rack", "expert"), None),
        P("rack", "expert", None, None, None),
        P("rack", "expert", None, None),
    )
    out_specs = P(("rack", "expert"), None)
    return jax.shard_map(
        functools.partial(per_device, grid),
        mesh=mesh, in_specs=in_specs, out_specs=out_specs, check_vma=False,
    )
```

```python
import functools

import jax
import jax.numpy as jnp
from jax import lax
from jax.experimental import pallas as pl
from jax.experimental.pallas import tpu as pltpu
from jax.sharding import PartitionSpec as P

MESH = pl.DeviceIdType.MESH
BF16 = jnp.bfloat16
F32 = jnp.float32
TILE = 128
GRID = (4, 8, 8)
ORDERS = (("y", "x", "z"), ("y", "z", "x"), ("z", "x", "y"))
STORED = ("z", "y", "x")
LONG = 8
SIDES = ((0, 1), (6, -1))
SEQUENCE = (0, 2, 1)
LANDING = (1, 0, 2)


def shares_of(tiles):
    first = (tiles + 1) // 3
    second = (tiles + 1 - first) // 2
    return (first - 1, second, tiles + 1 - first - second)


def kernel(
    grid, steps, top, experts, widths,
    hid_ref, gain_ref, ids_ref, lev_ref, wgu_ref, wd_ref, out_ref,
    ga, gb, gc, pa, pb, pc, gu_ref, act_ref, xs_ref, xr_ref,
    res_ref, mix_ref, mixs_ref, mixr_ref, hs_ref, hr_ref, fs_ref, fr_ref, sss_ref, ssr_ref,
    rr_a, rr_b, rr_c, st_a, st_b, st_c, u_a, u_b, u_c, v_a, v_b, v_c, w_a, w_b, w_c, t_a, t_b, t_c,
    ag_send, ag_recv, rs_send, rs_recv, pair_send, pair_recv,
):
    size = dict(zip("xyz", grid))
    rack, col = lax.axis_index("rack"), lax.axis_index("expert")
    here = {"x": rack // size["y"], "y": rack % size["y"], "z": col // 2}
    core = col % 2
    half = sum(widths)
    tokens = 2 * grid[0] * grid[1] * grid[2]
    starts = (0, widths[0], widths[0] + widths[1])
    gathered, partial = (ga, gb, gc), (pa, pb, pc)
    ring_in, ring_out = (rr_a, rr_b, rr_c), (st_a, st_b, st_c)
    mid_out, mid_in = (u_a, u_b, u_c), (v_a, v_b, v_c)
    last_out, last_in = (w_a, w_b, w_c), (t_a, t_b, t_c)

    def device(at):
        return (at["x"] * size["y"] + at["y"], at["z"] * 2 + core)

    def away(axis, shift):
        n = size[axis]
        return lax.rem(here[axis] + (shift + n) % n, n)

    def moved(axis, shift):
        return device({**here, axis: away(axis, shift)})

    mate = (rack, col + 1 - 2 * core)

    def span(names, part):
        lead = [a for a in STORED if a in names][:1]
        spans = {a: pl.ds(0, size[a]) for a in names}
        if part is not None:
            long = size[lead[0]] // 2
            spans[lead[0]] = pl.ds(part * long, long)
        return spans

    def where_at(full, axis=None, at=None, part=None):
        spans = span(full, part)
        return tuple(spans[a] if a in full else (at if a == axis else here[a]) for a in STORED)

    def inner(full, part=None):
        spans = span(full, part)
        return tuple(spans[a] for a in STORED if a in full)

    def to_mate(src, dst, slot):
        return pltpu.make_async_remote_copy(
            src_ref=src, dst_ref=dst, send_sem=pair_send.at[slot], recv_sem=pair_recv.at[slot],
            device_id=mate, device_id_type=MESH,
        )

    barrier = pltpu.get_barrier_semaphore()
    partners = [mate] + [moved(a, d) for a in "xyz" for d in range(1, size[a])]
    for partner in partners:
        pl.semaphore_signal(barrier, inc=1, device_id=partner, device_id_type=MESH)

    own = hid_ref[...].astype(F32)
    low, high = own[:, :half], own[:, half:]
    first_core = core == 0
    hs_ref[...] = jnp.where(first_core, high, low)
    levels = lev_ref[...].astype(F32)
    shares = levels / jnp.sum(levels, axis=-1, keepdims=True)
    chosen = ids_ref[...]
    lanes = lax.broadcasted_iota(jnp.int32, (steps, TILE), 1)
    mixing = jnp.zeros((steps, TILE), F32)
    for k in range(top):
        mixing += jnp.where(lanes == chosen[:, k : k + 1], shares[:, k : k + 1], 0.0)
    mixs_ref[...] = mixing
    pl.semaphore_wait(barrier, len(partners))
    sent = [to_mate(hs_ref, hr_ref, 0), to_mate(mixs_ref, mixr_ref, 1)]
    for copy in sent:
        copy.start()
    for copy in sent:
        copy.wait()
    row = lax.broadcasted_iota(jnp.int32, (2, half), 0)
    res_ref[...] = jnp.where(row == core, jnp.where(first_core, low, high), hr_ref[...])
    mix_row = lax.broadcasted_iota(jnp.int32, (2, TILE), 0)
    for s in range(steps):
        mix_ref[s] = jnp.where(mix_row == core, mixing[s : s + 1], mixr_ref[s : s + 1, :])
    gains = gain_ref[...]
    gain = jnp.where(first_core, gains[:, :half], gains[:, half:])

    def ag_copy(o, phase, slot, axis, full, at, shift, part=None):
        ref = gathered[o].at[where_at(full, axis, at, part)]
        return pltpu.make_async_remote_copy(
            src_ref=ref, dst_ref=ref, send_sem=ag_send.at[o, phase, slot],
            recv_sem=ag_recv.at[o, phase, slot], device_id=moved(axis, shift), device_id_type=MESH,
        )

    def rs_copy(o, phase, slot, src, dst, axis, shift):
        return pltpu.make_async_remote_copy(
            src_ref=src, dst_ref=dst, send_sem=rs_send.at[o, phase, slot],
            recv_sem=rs_recv.at[o, phase, slot], device_id=moved(axis, shift), device_id_type=MESH,
        )

    def one_step(step, carry):
        residual = res_ref[...]
        sss_ref[...] = jnp.broadcast_to(
            jnp.sum(residual * residual, axis=-1, keepdims=True), sss_ref.shape
        )
        copy = to_mate(sss_ref, ssr_ref, 2)
        copy.start()
        copy.wait()
        total = (sss_ref[...] + ssr_ref[...])[:, :1]
        normed = (residual * lax.rsqrt(total / (2 * half) + 1e-6) * gain).astype(BF16)
        for o in range(3):
            block = normed[:, starts[o] : starts[o] + widths[o]]
            if o == 0:
                block = jnp.concatenate([block, mix_ref[step].astype(BF16)], axis=1)
            gathered[o][where_at(())] = block

        sends = []

        def begin(copies):
            for copy in copies.values():
                copy.start()
            sends.extend(copies.values())
            return copies

        waits = {}
        for phase in range(2):
            for o in SEQUENCE:
                for copy in waits.get(o, {}).values():
                    copy.wait_recv()
                axis, full = ORDERS[o][phase], ORDERS[o][:phase]
                far = sorted(range(1, size[axis]), key=lambda d: -min(d, size[axis] - d))
                waits[o] = begin(
                    {d: ag_copy(o, phase, d - 1, axis, full, here[axis], d) for d in far}
                )
        for o in SEQUENCE:
            for copy in waits[o].values():
                copy.wait_recv()
            axis, full = ORDERS[o][2], ORDERS[o][:2]
            if size[axis] < LONG:
                waits[o] = begin({
                    d: ag_copy(o, 2, d - 1, axis, full, here[axis], d)
                    for d in range(1, size[axis])
                })
                continue
            copies = {}
            for part in range(2):
                for base, sign in SIDES:
                    copies[sign, 2, part] = ag_copy(
                        o, 2, base + part, axis, full, here[axis], 2 * sign, part
                    )
            for base, sign in SIDES:
                copies[sign, 1] = ag_copy(o, 2, base + 2, axis, full, here[axis], sign)
            waits[o] = begin(copies)
        for o in SEQUENCE:
            axis, full = ORDERS[o][2], ORDERS[o][:2]
            if size[axis] < LONG:
                continue
            for part in range(2):
                for base, sign in SIDES:
                    waits[o].pop((sign, 2, part)).wait_recv()
                    at = away(axis, -2 * sign)
                    copies = {}
                    if base == 6 * part:
                        copies[sign, 4] = ag_copy(o, 2, base + 5, axis, full, at, 2 * sign, part)
                    copies[sign, 3, part] = ag_copy(o, 2, base + 3 + part, axis, full, at, sign, part)
                    waits[o].update(begin(copies))

        chunk = tokens // size["z"]
        swaps = []
        for place, o in enumerate(LANDING):
            for copy in waits[o].values():
                copy.wait_recv()
            for z in range(size["z"]):
                rows = pl.ds(z * chunk, chunk)
                x = gathered[o][z].reshape(chunk, gathered[o].shape[-1])[:, : widths[o]]
                total = jnp.dot(
                    x, wgu_ref[starts[o] : starts[o] + widths[o], :], preferred_element_type=F32
                )
                if place:
                    total += gu_ref[rows, :]
                gu_ref[rows, :] = total
                if place == 2:
                    xs_ref[rows, :] = total.astype(BF16)
                    swap = to_mate(xs_ref.at[rows], xr_ref.at[rows], 3 + z)
                    swap.start()
                    swaps.append(swap)
        hidden = wd_ref.shape[0]
        mine = (
            lax.broadcasted_iota(jnp.int32, (tokens, TILE), 1) == rack
        )
        weight = jnp.sum(
            jnp.where(mine, ga[..., widths[0] :].reshape(tokens, TILE).astype(F32), 0.0),
            axis=-1, keepdims=True,
        )
        for z in range(size["z"]):
            rows = pl.ds(z * chunk, chunk)
            swaps[z].wait()
            both = gu_ref[rows, :] + xr_ref[rows, :].astype(F32)
            gate, up = both[:, :hidden], both[:, hidden:]
            act_ref[rows, :] = (gate / (1.0 + jnp.exp(-gate)) * up).astype(BF16)
        for copy in sends:
            copy.wait_send()

        sends = []
        waits = {}
        for o in SEQUENCE:
            part = jnp.dot(
                act_ref[...], wd_ref[:, starts[o] : starts[o] + widths[o]],
                preferred_element_type=F32,
            )
            partial[o][...] = (part * weight).astype(BF16).reshape(partial[o].shape)
            axis, full = ORDERS[o][2], ORDERS[o][:2]
            if size[axis] < LONG:
                waits[o] = begin({
                    d: rs_copy(
                        o, 0, d - 1, partial[o].at[where_at(full, axis, away(axis, d))],
                        ring_in[o].at[d - 1], axis, d,
                    )
                    for d in range(1, size[axis])
                })
                continue
            copies = {}
            for side, (base, sign) in enumerate(SIDES):
                copies[sign, 4] = rs_copy(
                    o, 0, base + 2, partial[o].at[where_at(full, axis, away(axis, 4 * sign), side)],
                    ring_in[o].at[(side, 1) + inner(full, side)], axis, 2 * sign,
                )
            for half_part in range(2):
                for side, (base, sign) in enumerate(SIDES):
                    p = half_part if side == 0 else 1 - half_part
                    copies[sign, 3, p] = rs_copy(
                        o, 0, base + p,
                        partial[o].at[where_at(full, axis, away(axis, 3 * sign), p)],
                        ring_in[o].at[(side, 0) + inner(full, p)], axis, sign,
                    )
            for side, (base, sign) in enumerate(SIDES):
                copies[sign, 1] = rs_copy(
                    o, 0, base + 3, partial[o].at[where_at(full, axis, away(axis, sign))],
                    ring_in[o].at[side, 2], axis, sign,
                )
            waits[o] = begin(copies)
        for o in SEQUENCE:
            axis, full = ORDERS[o][2], ORDERS[o][:2]
            if size[axis] < LONG:
                continue
            for half_part in range(2):
                for side, (base, sign) in enumerate(SIDES):
                    p = half_part if side == 0 else 1 - half_part
                    block = inner(full, p)
                    waits[o].pop((sign, 3, p)).wait_recv()
                    total = partial[o][where_at(full, axis, away(axis, 2 * sign), p)].astype(F32)
                    total += ring_in[o][(side, 0) + block].astype(F32)
                    if p == side:
                        waits[o].pop((sign, 4)).wait_recv()
                        total += ring_in[o][(side, 1) + block].astype(F32)
                    ring_out[o][(side,) + block] = total.astype(BF16)
                    waits[o].update(begin({(sign, 2, p): rs_copy(
                        o, 0, base + 4 + p, ring_out[o].at[(side,) + block],
                        ring_in[o].at[(side, 3) + block], axis, 2 * sign,
                    )}))
        flying = {}
        for o in LANDING:
            axis, full = ORDERS[o][2], ORDERS[o][:2]
            for copy in waits[o].values():
                copy.wait_recv()
            total = partial[o][where_at(full, axis, here[axis])].astype(F32)
            if size[axis] < LONG:
                for d in range(1, size[axis]):
                    total += ring_in[o][d - 1].astype(F32)
            else:
                for side in range(2):
                    total += ring_in[o][side, 2].astype(F32) + ring_in[o][side, 3].astype(F32)
            mid_out[o][...] = total.astype(BF16)
            axis = ORDERS[o][1]
            copies = {}
            for d in range(1, size[axis]):
                at = tuple(away(axis, d) if a == axis else pl.ds(0, size[a]) for a in STORED if a in full)
                copies[d] = rs_copy(o, 1, d - 1, mid_out[o].at[at], mid_in[o].at[d - 1], axis, d)
            flying[o] = begin(copies)
        waits = flying
        flying = {}
        for o in LANDING:
            axis, full = ORDERS[o][1], ORDERS[o][:2]
            at = tuple(here[axis] if a == axis else pl.ds(0, size[a]) for a in STORED if a in full)
            total = mid_out[o][at].astype(F32)
            for d in range(1, size[axis]):
                waits[o][d].wait_recv()
                total += mid_in[o][d - 1].astype(F32)
            last_out[o][...] = total.astype(BF16)
            axis = ORDERS[o][0]
            flying[o] = begin({
                d: rs_copy(o, 2, d - 1, last_out[o].at[away(axis, d)], last_in[o].at[d - 1], axis, d)
                for d in range(1, size[axis])
            })
        waits = flying
        for o in LANDING:
            axis = ORDERS[o][0]
            total = last_out[o][here[axis]].astype(F32)
            for d in range(1, size[axis]):
                waits[o][d].wait_recv()
                total += last_in[o][d - 1].astype(F32)
            res_ref[:, starts[o] : starts[o] + widths[o]] += total
        for copy in sends:
            copy.wait_send()
        return carry

    lax.fori_loop(0, steps, one_step, 0)

    residual = res_ref[...]
    fs_ref[...] = jnp.where(first_core, residual[1:2], residual[0:1])
    copy = to_mate(fs_ref, fr_ref, 2)
    copy.start()
    kept = jnp.where(first_core, residual[0:1], residual[1:2])
    copy.wait()
    out_ref[:, :half] = jnp.where(first_core, kept, fr_ref[...])
    out_ref[:, half:] = jnp.where(first_core, fr_ref[...], kept)


def per_device(grid, hidden_in, norm_gain, expert_ids, gate_levels, w_gate_up, w_down):
    steps, _, top = expert_ids.shape
    width = hidden_in.shape[1]
    half = width // 2
    hidden = w_down.shape[2]
    tokens = 2 * grid[0] * grid[1] * grid[2]
    widths = tuple(TILE * n for n in shares_of(half // TILE))
    size = dict(zip("xyz", grid))
    stored = tuple(size[a] for a in STORED)

    def dims(names):
        return tuple(size[a] for a in STORED if a in names)

    scratch = [pltpu.VMEM(stored + (2, w + (TILE if o == 0 else 0)), BF16) for o, w in enumerate(widths)]
    scratch += [pltpu.VMEM(stored + (2, w), BF16) for w in widths]
    scratch += [
        pltpu.VMEM((tokens, 2 * hidden), F32),
        pltpu.VMEM((tokens, hidden), BF16),
        pltpu.VMEM((tokens, 2 * hidden), BF16),
        pltpu.VMEM((tokens, 2 * hidden), BF16),
        pltpu.VMEM((2, half), F32),
        pltpu.VMEM((steps, 2, TILE), F32),
        pltpu.VMEM((steps, TILE), F32),
        pltpu.VMEM((steps, TILE), F32),
        pltpu.VMEM((1, half), F32),
        pltpu.VMEM((1, half), F32),
        pltpu.VMEM((1, half), F32),
        pltpu.VMEM((1, half), F32),
        pltpu.VMEM((2, TILE), F32),
        pltpu.VMEM((2, TILE), F32),
    ]
    lines = [(2, 4) if size[o[2]] >= LONG else (size[o[2]] - 1,) for o in ORDERS]
    scratch += [
        pltpu.VMEM(n + dims(o[:2]) + (2, w), BF16) for n, o, w in zip(lines, ORDERS, widths)
    ]
    scratch += [pltpu.VMEM((2,) + dims(o[:2]) + (2, w), BF16) for o, w in zip(ORDERS, widths)]
    scratch += [pltpu.VMEM(dims(o[:2]) + (2, w), BF16) for o, w in zip(ORDERS, widths)]
    scratch += [
        pltpu.VMEM((size[o[1]] - 1, size[o[0]], 2, w), BF16) for o, w in zip(ORDERS, widths)
    ]
    scratch += [pltpu.VMEM((size[o[0]], 2, w), BF16) for o, w in zip(ORDERS, widths)]
    scratch += [pltpu.VMEM((size[o[0]] - 1, 2, w), BF16) for o, w in zip(ORDERS, widths)]
    most = 12
    scratch += [pltpu.SemaphoreType.DMA((3, 3, most))] * 4
    scratch += [pltpu.SemaphoreType.DMA((3 + size["z"],))] * 2
    return pl.pallas_call(
        functools.partial(kernel, grid, steps, top, 0, widths),
        out_shape=jax.ShapeDtypeStruct((1, width), F32),
        in_specs=[pl.BlockSpec(memory_space=pltpu.VMEM)] * 6,
        out_specs=pl.BlockSpec(memory_space=pltpu.VMEM),
        scratch_shapes=scratch,
        compiler_params=pltpu.CompilerParams(
            collective_id=0, has_side_effects=True, vmem_limit_bytes=48 << 20
        ),
    )(
        hidden_in,
        norm_gain.reshape(1, width),
        expert_ids[:, 0, :],
        gate_levels[:, 0, :],
        w_gate_up[0, 0].reshape(half, 2 * hidden),
        w_down[0, 0],
    )


def solution(mesh, grid=GRID):
    in_specs = (
        P(("rack", "expert"), None),
        P(),
        P(None, ("rack", "expert"), None),
        P(None, ("rack", "expert"), None),
        P("rack", "expert", None, None, None),
        P("rack", "expert", None, None),
    )
    out_specs = P(("rack", "expert"), None)
    return jax.shard_map(
        functools.partial(per_device, grid),
        mesh=mesh, in_specs=in_specs, out_specs=out_specs, check_vma=False,
    )
```

```python
import functools

import jax
import jax.numpy as jnp
from jax import lax
from jax.experimental import pallas as pl
from jax.experimental.pallas import tpu as pltpu
from jax.sharding import PartitionSpec as P

MESH = pl.DeviceIdType.MESH
BF16 = jnp.bfloat16
F32 = jnp.float32
TILE = 128
GRID = (4, 8, 8)
ORDERS = (("y", "x", "z"), ("y", "z", "x"), ("z", "x", "y"))
STORED = ("z", "y", "x")
LONG = 8
SIDES = ((0, 1), (6, -1))
SEQUENCE = (0, 2, 1)
LANDING = (1, 0, 2)
TAGGED = LANDING[-1]


def shares_of(tiles):
    first = (tiles + 1) // 3
    second = (tiles + 1 - first) // 2
    return (first, second, tiles - first - second)


def kernel(
    grid, steps, top, widths,
    hid_ref, gain_ref, ids_ref, lev_ref, wgu_ref, wd_ref, out_ref,
    ga, gb, gc, pa, pb, pc, gu_ref, act_ref, xs_ref, xr_ref,
    res_ref, mix_ref, mixs_ref, mixr_ref, hs_ref, hr_ref, fs_ref, fr_ref, tag_ref,
    rr_a, rr_b, rr_c, st_a, st_b, st_c, u_a, u_b, u_c, v_a, v_b, v_c, w_a, w_b, w_c, t_a, t_b, t_c,
    ag_send, ag_recv, rs_send, rs_recv, pair_send, pair_recv,
):
    size = dict(zip("xyz", grid))
    rack, col = lax.axis_index("rack"), lax.axis_index("expert")
    here = {"x": rack // size["y"], "y": rack % size["y"], "z": col // 2}
    core = col % 2
    half = sum(widths)
    experts = grid[0] * grid[1]
    tokens = 2 * grid[0] * grid[1] * grid[2]
    starts = (0, widths[0], widths[0] + widths[1])
    gathered, partial = (ga, gb, gc), (pa, pb, pc)
    ring_in, ring_out = (rr_a, rr_b, rr_c), (st_a, st_b, st_c)
    mid_out, mid_in = (u_a, u_b, u_c), (v_a, v_b, v_c)
    last_out, last_in = (w_a, w_b, w_c), (t_a, t_b, t_c)

    def device(at):
        return (at["x"] * size["y"] + at["y"], at["z"] * 2 + core)

    def away(axis, shift):
        n = size[axis]
        return lax.rem(here[axis] + (shift + n) % n, n)

    def moved(axis, shift):
        return device({**here, axis: away(axis, shift)})

    mate = (rack, col + 1 - 2 * core)

    def span(names, part):
        lead = [a for a in STORED if a in names][:1]
        spans = {a: pl.ds(0, size[a]) for a in names}
        if part is not None:
            long = size[lead[0]] // 2
            spans[lead[0]] = pl.ds(part * long, long)
        return spans

    def where_at(full, axis=None, at=None, part=None):
        spans = span(full, part)
        return tuple(spans[a] if a in full else (at if a == axis else here[a]) for a in STORED)

    def inner(full, part=None):
        spans = span(full, part)
        return tuple(spans[a] for a in STORED if a in full)

    def to_mate(src, dst, slot, turn=0):
        return pltpu.make_async_remote_copy(
            src_ref=src, dst_ref=dst, send_sem=pair_send.at[turn, slot],
            recv_sem=pair_recv.at[turn, slot],
            device_id=mate, device_id_type=MESH,
        )

    barrier = pltpu.get_barrier_semaphore()
    partners = [mate] + [moved(a, d) for a in "xyz" for d in range(1, size[a])]
    for partner in partners:
        pl.semaphore_signal(barrier, inc=1, device_id=partner, device_id_type=MESH)

    own = hid_ref[...].astype(F32)
    low, high = own[:, :half], own[:, half:]
    first_core = core == 0
    hs_ref[...] = jnp.where(first_core, high, low)
    levels = lev_ref[...].astype(F32)
    shares = levels / jnp.sum(levels, axis=-1, keepdims=True)
    chosen = ids_ref[...]
    lanes = lax.broadcasted_iota(jnp.int32, (steps, TILE), 1)
    mixing = jnp.zeros((steps, TILE), F32)
    for k in range(top):
        mixing += jnp.where(lanes == chosen[:, k : k + 1], shares[:, k : k + 1], 0.0)
    mixs_ref[...] = mixing
    pl.semaphore_wait(barrier, len(partners))
    sent = [to_mate(hs_ref, hr_ref, 0), to_mate(mixs_ref, mixr_ref, 1)]
    for copy in sent:
        copy.start()
    for copy in sent:
        copy.wait()
    row = lax.broadcasted_iota(jnp.int32, (2, half), 0)
    res_ref[...] = jnp.where(row == core, jnp.where(first_core, low, high), hr_ref[...])
    mix_row = lax.broadcasted_iota(jnp.int32, (2, TILE), 0)
    for s in range(steps):
        mix_ref[s] = jnp.where(mix_row == core, mixing[s : s + 1], mixr_ref[s : s + 1, :])
    gains = gain_ref[...]
    gain = jnp.where(first_core, gains[:, :half], gains[:, half:])

    def ag_copy(o, phase, slot, axis, full, at, shift, part=None):
        ref = gathered[o].at[where_at(full, axis, at, part)]
        return pltpu.make_async_remote_copy(
            src_ref=ref, dst_ref=ref, send_sem=ag_send.at[o, phase, slot],
            recv_sem=ag_recv.at[o, phase, slot], device_id=moved(axis, shift), device_id_type=MESH,
        )

    def rs_copy(o, phase, slot, src, dst, axis, shift):
        return pltpu.make_async_remote_copy(
            src_ref=src, dst_ref=dst, send_sem=rs_send.at[o, phase, slot],
            recv_sem=rs_recv.at[o, phase, slot], device_id=moved(axis, shift), device_id_type=MESH,
        )

    def first_copies(o):
        axis = ORDERS[o][0]
        far = sorted(range(1, size[axis]), key=lambda d: -min(d, size[axis] - d))
        return {d: ag_copy(o, 0, d - 1, axis, (), here[axis], d) for d in far}

    def send_share(o, step):
        cols = slice(starts[o], starts[o] + widths[o])
        block = (res_ref[:, cols] * gain[:, cols]).astype(BF16)
        if o == TAGGED:
            residual = res_ref[...]
            square = jnp.sum(residual * residual, axis=-1, keepdims=True)
            tag = mix_ref[step]
            lane = lax.broadcasted_iota(jnp.int32, (2, TILE), 1)
            for n in range(3):
                piece = square.astype(BF16).astype(F32)
                tag = jnp.where(lane == experts + n, piece, tag)
                square = square - piece
            block = jnp.concatenate([block, tag.astype(BF16)], axis=1)
        gathered[o][where_at(())] = block
        for copy in first_copies(o).values():
            copy.start()

    for o in LANDING:
        send_share(o, 0)

    def one_step(step, carry):
        turn = lax.rem(step, 2)
        sends = []

        def begin(copies):
            for copy in copies.values():
                copy.start()
            sends.extend(copies.values())
            return copies

        waits = {o: first_copies(o) for o in range(3)}
        for o in LANDING:
            sends.extend(waits[o].values())
        for o in LANDING:
            for copy in waits[o].values():
                copy.wait_recv()
            axis, full = ORDERS[o][1], ORDERS[o][:1]
            far = sorted(range(1, size[axis]), key=lambda d: -min(d, size[axis] - d))
            waits[o] = begin({d: ag_copy(o, 1, d - 1, axis, full, here[axis], d) for d in far})
        for o in SEQUENCE:
            for copy in waits[o].values():
                copy.wait_recv()
            axis, full = ORDERS[o][2], ORDERS[o][:2]
            if size[axis] < LONG:
                waits[o] = begin({
                    d: ag_copy(o, 2, d - 1, axis, full, here[axis], d)
                    for d in range(1, size[axis])
                })
                continue
            copies = {}
            for part in range(2):
                for base, sign in SIDES:
                    copies[sign, 2, part] = ag_copy(
                        o, 2, base + part, axis, full, here[axis], 2 * sign, part
                    )
            for base, sign in SIDES:
                copies[sign, 1] = ag_copy(o, 2, base + 2, axis, full, here[axis], sign)
            waits[o] = begin(copies)
        for o in SEQUENCE:
            axis, full = ORDERS[o][2], ORDERS[o][:2]
            if size[axis] < LONG:
                continue
            for part in range(2):
                for base, sign in SIDES:
                    waits[o].pop((sign, 2, part)).wait_recv()
                    at = away(axis, -2 * sign)
                    copies = {}
                    if base == 6 * part:
                        copies[sign, 4] = ag_copy(o, 2, base + 5, axis, full, at, 2 * sign, part)
                    copies[sign, 3, part] = ag_copy(o, 2, base + 3 + part, axis, full, at, sign, part)
                    waits[o].update(begin(copies))

        chunk = tokens // size["z"]
        swaps = []
        for place, o in enumerate(LANDING):
            for copy in waits[o].values():
                copy.wait_recv()
            if o == TAGGED:
                spot = (slice(None),) * 4 + (pl.ds(widths[o], TILE),)
                told = to_mate(gathered[o].at[spot], tag_ref.at[turn], 3 + size["z"], turn)
                told.start()
            for z in range(size["z"]):
                rows = pl.ds(z * chunk, chunk)
                x = gathered[o][z].reshape(chunk, gathered[o].shape[-1])[:, : widths[o]]
                total = jnp.dot(
                    x, wgu_ref[starts[o] : starts[o] + widths[o], :], preferred_element_type=F32
                )
                if place:
                    total += gu_ref[rows, :]
                gu_ref[rows, :] = total
                if place == 2:
                    xs_ref[rows, :] = total.astype(BF16)
                    swap = to_mate(xs_ref.at[rows], xr_ref.at[turn, rows], 3 + z, turn)
                    swap.start()
                    swaps.append(swap)
        hidden = wd_ref.shape[0]
        lane = lax.broadcasted_iota(jnp.int32, (tokens, TILE), 1)
        square = (lane >= experts) & (lane < experts + 3)

        def picked(tag, mask):
            return jnp.sum(jnp.where(mask, tag, 0.0), axis=-1, keepdims=True)

        tag = gathered[TAGGED][..., widths[TAGGED] :].reshape(tokens, TILE).astype(F32)
        weight = picked(tag, lane == rack)
        told.wait()
        total = picked(tag, square) + picked(tag_ref[turn].reshape(tokens, TILE).astype(F32), square)
        scale = lax.rsqrt(total / (2 * half) + 1e-6)
        for z in range(size["z"]):
            rows = pl.ds(z * chunk, chunk)
            swaps[z].wait()
            both = gu_ref[rows, :] + xr_ref[turn, rows, :].astype(F32)
            both = both * scale[z * chunk : (z + 1) * chunk]
            gate, up = both[:, :hidden], both[:, hidden:]
            act_ref[rows, :] = (gate / (1.0 + jnp.exp(-gate)) * up).astype(BF16)
        for copy in sends:
            copy.wait_send()

        sends = []
        waits = {}
        for o in SEQUENCE:
            part = jnp.dot(
                act_ref[...], wd_ref[:, starts[o] : starts[o] + widths[o]],
                preferred_element_type=F32,
            )
            partial[o][...] = (part * weight).astype(BF16).reshape(partial[o].shape)
            axis, full = ORDERS[o][2], ORDERS[o][:2]
            if size[axis] < LONG:
                waits[o] = begin({
                    d: rs_copy(
                        o, 0, d - 1, partial[o].at[where_at(full, axis, away(axis, d))],
                        ring_in[o].at[d - 1], axis, d,
                    )
                    for d in range(1, size[axis])
                })
                continue
            copies = {}
            for side, (base, sign) in enumerate(SIDES):
                copies[sign, 4] = rs_copy(
                    o, 0, base + 2, partial[o].at[where_at(full, axis, away(axis, 4 * sign), side)],
                    ring_in[o].at[(side, 1) + inner(full, side)], axis, 2 * sign,
                )
            for half_part in range(2):
                for side, (base, sign) in enumerate(SIDES):
                    p = half_part if side == 0 else 1 - half_part
                    copies[sign, 3, p] = rs_copy(
                        o, 0, base + p,
                        partial[o].at[where_at(full, axis, away(axis, 3 * sign), p)],
                        ring_in[o].at[(side, 0) + inner(full, p)], axis, sign,
                    )
            for side, (base, sign) in enumerate(SIDES):
                copies[sign, 1] = rs_copy(
                    o, 0, base + 3, partial[o].at[where_at(full, axis, away(axis, sign))],
                    ring_in[o].at[side, 2], axis, sign,
                )
            waits[o] = begin(copies)
        for o in SEQUENCE:
            axis, full = ORDERS[o][2], ORDERS[o][:2]
            if size[axis] < LONG:
                continue
            for half_part in range(2):
                for side, (base, sign) in enumerate(SIDES):
                    p = half_part if side == 0 else 1 - half_part
                    block = inner(full, p)
                    waits[o].pop((sign, 3, p)).wait_recv()
                    total = partial[o][where_at(full, axis, away(axis, 2 * sign), p)].astype(F32)
                    total += ring_in[o][(side, 0) + block].astype(F32)
                    if p == side:
                        waits[o].pop((sign, 4)).wait_recv()
                        total += ring_in[o][(side, 1) + block].astype(F32)
                    ring_out[o][(side,) + block] = total.astype(BF16)
                    waits[o].update(begin({(sign, 2, p): rs_copy(
                        o, 0, base + 4 + p, ring_out[o].at[(side,) + block],
                        ring_in[o].at[(side, 3) + block], axis, 2 * sign,
                    )}))
        flying = {}
        for o in LANDING:
            axis, full = ORDERS[o][2], ORDERS[o][:2]
            for copy in waits[o].values():
                copy.wait_recv()
            total = partial[o][where_at(full, axis, here[axis])].astype(F32)
            if size[axis] < LONG:
                for d in range(1, size[axis]):
                    total += ring_in[o][d - 1].astype(F32)
            else:
                for side in range(2):
                    total += ring_in[o][side, 2].astype(F32) + ring_in[o][side, 3].astype(F32)
            mid_out[o][...] = total.astype(BF16)
            axis = ORDERS[o][1]
            copies = {}
            for d in range(1, size[axis]):
                at = tuple(away(axis, d) if a == axis else pl.ds(0, size[a]) for a in STORED if a in full)
                copies[d] = rs_copy(o, 1, d - 1, mid_out[o].at[at], mid_in[o].at[d - 1], axis, d)
            flying[o] = begin(copies)
        waits = flying
        flying = {}
        for o in LANDING:
            axis, full = ORDERS[o][1], ORDERS[o][:2]
            at = tuple(here[axis] if a == axis else pl.ds(0, size[a]) for a in STORED if a in full)
            total = mid_out[o][at].astype(F32)
            for d in range(1, size[axis]):
                waits[o][d].wait_recv()
                total += mid_in[o][d - 1].astype(F32)
            last_out[o][...] = total.astype(BF16)
            axis = ORDERS[o][0]
            flying[o] = begin({
                d: rs_copy(o, 2, d - 1, last_out[o].at[away(axis, d)], last_in[o].at[d - 1], axis, d)
                for d in range(1, size[axis])
            })
        waits = flying
        for o in LANDING:
            axis = ORDERS[o][0]
            total = last_out[o][here[axis]].astype(F32)
            for d in range(1, size[axis]):
                waits[o][d].wait_recv()
                total += last_in[o][d - 1].astype(F32)
            res_ref[:, starts[o] : starts[o] + widths[o]] += total

            @pl.when(step < steps - 1)
            def _(o=o):
                send_share(o, step + 1)

        for copy in sends:
            copy.wait_send()
        return carry

    lax.fori_loop(0, steps, one_step, 0)

    residual = res_ref[...]
    fs_ref[...] = jnp.where(first_core, residual[1:2], residual[0:1])
    copy = to_mate(fs_ref, fr_ref, 2)
    copy.start()
    kept = jnp.where(first_core, residual[0:1], residual[1:2])
    copy.wait()
    out_ref[:, :half] = jnp.where(first_core, kept, fr_ref[...])
    out_ref[:, half:] = jnp.where(first_core, fr_ref[...], kept)


def per_device(grid, hidden_in, norm_gain, expert_ids, gate_levels, w_gate_up, w_down):
    steps, _, top = expert_ids.shape
    width = hidden_in.shape[1]
    half = width // 2
    hidden = w_down.shape[2]
    tokens = 2 * grid[0] * grid[1] * grid[2]
    widths = tuple(TILE * n for n in shares_of(half // TILE))
    size = dict(zip("xyz", grid))
    stored = tuple(size[a] for a in STORED)

    def dims(names):
        return tuple(size[a] for a in STORED if a in names)

    scratch = [pltpu.VMEM(stored + (2, w + (TILE if o == TAGGED else 0)), BF16) for o, w in enumerate(widths)]
    scratch += [pltpu.VMEM(stored + (2, w), BF16) for w in widths]
    scratch += [
        pltpu.VMEM((tokens, 2 * hidden), F32),
        pltpu.VMEM((tokens, hidden), BF16),
        pltpu.VMEM((tokens, 2 * hidden), BF16),
        pltpu.VMEM((2, tokens, 2 * hidden), BF16),
        pltpu.VMEM((2, half), F32),
        pltpu.VMEM((steps, 2, TILE), F32),
        pltpu.VMEM((steps, TILE), F32),
        pltpu.VMEM((steps, TILE), F32),
        pltpu.VMEM((1, half), F32),
        pltpu.VMEM((1, half), F32),
        pltpu.VMEM((1, half), F32),
        pltpu.VMEM((1, half), F32),
        pltpu.VMEM((2,) + stored + (2, TILE), BF16),
    ]
    lines = [(2, 4) if size[o[2]] >= LONG else (size[o[2]] - 1,) for o in ORDERS]
    scratch += [
        pltpu.VMEM(n + dims(o[:2]) + (2, w), BF16) for n, o, w in zip(lines, ORDERS, widths)
    ]
    scratch += [pltpu.VMEM((2,) + dims(o[:2]) + (2, w), BF16) for o, w in zip(ORDERS, widths)]
    scratch += [pltpu.VMEM(dims(o[:2]) + (2, w), BF16) for o, w in zip(ORDERS, widths)]
    scratch += [
        pltpu.VMEM((size[o[1]] - 1, size[o[0]], 2, w), BF16) for o, w in zip(ORDERS, widths)
    ]
    scratch += [pltpu.VMEM((size[o[0]], 2, w), BF16) for o, w in zip(ORDERS, widths)]
    scratch += [pltpu.VMEM((size[o[0]] - 1, 2, w), BF16) for o, w in zip(ORDERS, widths)]
    most = 12
    scratch += [pltpu.SemaphoreType.DMA((3, 3, most))] * 4
    scratch += [pltpu.SemaphoreType.DMA((2, 4 + size["z"]))] * 2
    return pl.pallas_call(
        functools.partial(kernel, grid, steps, top, widths),
        out_shape=jax.ShapeDtypeStruct((1, width), F32),
        in_specs=[pl.BlockSpec(memory_space=pltpu.VMEM)] * 6,
        out_specs=pl.BlockSpec(memory_space=pltpu.VMEM),
        scratch_shapes=scratch,
        compiler_params=pltpu.CompilerParams(
            collective_id=0, has_side_effects=True, vmem_limit_bytes=48 << 20
        ),
    )(
        hidden_in,
        norm_gain.reshape(1, width),
        expert_ids[:, 0, :],
        gate_levels[:, 0, :],
        w_gate_up[0, 0].reshape(half, 2 * hidden),
        w_down[0, 0],
    )


def solution(mesh, grid=GRID):
    in_specs = (
        P(("rack", "expert"), None),
        P(),
        P(None, ("rack", "expert"), None),
        P(None, ("rack", "expert"), None),
        P("rack", "expert", None, None, None),
        P("rack", "expert", None, None),
    )
    out_specs = P(("rack", "expert"), None)
    return jax.shard_map(
        functools.partial(per_device, grid),
        mesh=mesh, in_specs=in_specs, out_specs=out_specs, check_vma=False,
    )
```

```python
import functools

import jax
import jax.numpy as jnp
from jax import lax
from jax.experimental import pallas as pl
from jax.experimental.pallas import tpu as pltpu
from jax.sharding import PartitionSpec as P

MESH = pl.DeviceIdType.MESH
BF16 = jnp.bfloat16
F32 = jnp.float32
TILE = 128
GRID = (4, 8, 8)
ORDERS = (("y", "x", "z"), ("y", "z", "x"), ("z", "x", "y"))
STORED = ("z", "y", "x")
LONG = 8
SIDES = ((0, 1), (6, -1))
SEQUENCE = (0, 2, 1)
LANDING = (1, 0, 2)
TAGGED = LANDING[-1]


def shares_of(tiles):
    first = (tiles + 1) // 3
    second = (tiles + 1 - first) // 2
    return (first, second, tiles - first - second)


def kernel(
    grid, steps, top, widths,
    hid_ref, gain_ref, ids_ref, lev_ref, wgu_ref, wd_ref, out_ref,
    ga, gb, gc, pa, pb, pc, gu_ref, act_ref, xs_ref, xr_ref,
    res_ref, mix_ref, mixs_ref, mixr_ref, hs_ref, hr_ref, fs_ref, fr_ref, tag_ref,
    rr_a, rr_b, rr_c, st_a, st_b, st_c, u_a, u_b, u_c, v_a, v_b, v_c, w_a, w_b, w_c, t_a, t_b, t_c,
    ag_send, ag_recv, rs_send, rs_recv, pair_send, pair_recv,
):
    size = dict(zip("xyz", grid))
    rack, col = lax.axis_index("rack"), lax.axis_index("expert")
    here = {"x": rack // size["y"], "y": rack % size["y"], "z": col // 2}
    core = col % 2
    half = sum(widths)
    experts = grid[0] * grid[1]
    tokens = 2 * grid[0] * grid[1] * grid[2]
    starts = (0, widths[0], widths[0] + widths[1])
    gathered, partial = (ga, gb, gc), (pa, pb, pc)
    ring_in, ring_out = (rr_a, rr_b, rr_c), (st_a, st_b, st_c)
    mid_out, mid_in = (u_a, u_b, u_c), (v_a, v_b, v_c)
    last_out, last_in = (w_a, w_b, w_c), (t_a, t_b, t_c)

    def device(at):
        return (at["x"] * size["y"] + at["y"], at["z"] * 2 + core)

    def away(axis, shift):
        n = size[axis]
        return lax.rem(here[axis] + (shift + n) % n, n)

    def moved(axis, shift):
        return device({**here, axis: away(axis, shift)})

    mate = (rack, col + 1 - 2 * core)

    def span(names, part):
        lead = [a for a in STORED if a in names][:1]
        spans = {a: pl.ds(0, size[a]) for a in names}
        if part is not None:
            long = size[lead[0]] // 2
            spans[lead[0]] = pl.ds(part * long, long)
        return spans

    def where_at(full, axis=None, at=None, part=None):
        spans = span(full, part)
        return tuple(spans[a] if a in full else (at if a == axis else here[a]) for a in STORED)

    def inner(full, part=None):
        spans = span(full, part)
        return tuple(spans[a] for a in STORED if a in full)

    def to_mate(src, dst, slot, turn=0):
        return pltpu.make_async_remote_copy(
            src_ref=src, dst_ref=dst, send_sem=pair_send.at[turn, slot],
            recv_sem=pair_recv.at[turn, slot],
            device_id=mate, device_id_type=MESH,
        )

    barrier = pltpu.get_barrier_semaphore()
    partners = [mate] + [moved(a, d) for a in "xyz" for d in range(1, size[a])]
    for partner in partners:
        pl.semaphore_signal(barrier, inc=1, device_id=partner, device_id_type=MESH)

    own = hid_ref[...].astype(F32)
    low, high = own[:, :half], own[:, half:]
    first_core = core == 0
    hs_ref[...] = jnp.where(first_core, high, low)
    levels = lev_ref[...].astype(F32)
    shares = levels / jnp.sum(levels, axis=-1, keepdims=True)
    chosen = ids_ref[...]
    lanes = lax.broadcasted_iota(jnp.int32, (steps, TILE), 1)
    mixing = jnp.zeros((steps, TILE), F32)
    for k in range(top):
        mixing += jnp.where(lanes == chosen[:, k : k + 1], shares[:, k : k + 1], 0.0)
    mixs_ref[...] = mixing
    pl.semaphore_wait(barrier, len(partners))
    sent = [to_mate(hs_ref, hr_ref, 0), to_mate(mixs_ref, mixr_ref, 1)]
    for copy in sent:
        copy.start()
    for copy in sent:
        copy.wait()
    row = lax.broadcasted_iota(jnp.int32, (2, half), 0)
    res_ref[...] = jnp.where(row == core, jnp.where(first_core, low, high), hr_ref[...])
    mix_row = lax.broadcasted_iota(jnp.int32, (2, TILE), 0)
    for s in range(steps):
        mix_ref[s] = jnp.where(mix_row == core, mixing[s : s + 1], mixr_ref[s : s + 1, :])
    gains = gain_ref[...]
    gain = jnp.where(first_core, gains[:, :half], gains[:, half:])

    def ag_copy(o, phase, slot, axis, full, at, shift, part=None):
        ref = gathered[o].at[where_at(full, axis, at, part)]
        return pltpu.make_async_remote_copy(
            src_ref=ref, dst_ref=ref, send_sem=ag_send.at[o, phase, slot],
            recv_sem=ag_recv.at[o, phase, slot], device_id=moved(axis, shift), device_id_type=MESH,
        )

    def rs_copy(o, phase, slot, src, dst, axis, shift):
        return pltpu.make_async_remote_copy(
            src_ref=src, dst_ref=dst, send_sem=rs_send.at[o, phase, slot],
            recv_sem=rs_recv.at[o, phase, slot], device_id=moved(axis, shift), device_id_type=MESH,
        )

    def first_copies(o):
        axis = ORDERS[o][0]
        far = sorted(range(1, size[axis]), key=lambda d: -min(d, size[axis] - d))
        return {d: ag_copy(o, 0, d - 1, axis, (), here[axis], d) for d in far}

    def send_share(o, step):
        cols = slice(starts[o], starts[o] + widths[o])
        block = (res_ref[:, cols] * gain[:, cols]).astype(BF16)
        if o == TAGGED:
            residual = res_ref[...]
            square = jnp.sum(residual * residual, axis=-1, keepdims=True)
            tag = mix_ref[step]
            lane = lax.broadcasted_iota(jnp.int32, (2, TILE), 1)
            for n in range(3):
                piece = square.astype(BF16).astype(F32)
                tag = jnp.where(lane == experts + n, piece, tag)
                square = square - piece
            block = jnp.concatenate([block, tag.astype(BF16)], axis=1)
        gathered[o][where_at(())] = block
        for copy in first_copies(o).values():
            copy.start()

    for o in LANDING:
        send_share(o, 0)

    def one_step(step, carry):
        turn = lax.rem(step, 2)
        sends = []

        def begin(copies):
            for copy in copies.values():
                copy.start()
            sends.extend(copies.values())
            return copies

        waits = {o: first_copies(o) for o in range(3)}
        for o in LANDING:
            sends.extend(waits[o].values())
        for o in LANDING:
            for copy in waits[o].values():
                copy.wait_recv()
            axis, full = ORDERS[o][1], ORDERS[o][:1]
            far = sorted(range(1, size[axis]), key=lambda d: -min(d, size[axis] - d))
            waits[o] = begin({d: ag_copy(o, 1, d - 1, axis, full, here[axis], d) for d in far})
        for o in SEQUENCE:
            for copy in waits[o].values():
                copy.wait_recv()
            axis, full = ORDERS[o][2], ORDERS[o][:2]
            if size[axis] < LONG:
                waits[o] = begin({
                    d: ag_copy(o, 2, d - 1, axis, full, here[axis], d)
                    for d in range(1, size[axis])
                })
                continue
            copies = {}
            for part in range(2):
                for base, sign in SIDES:
                    copies[sign, 2, part] = ag_copy(
                        o, 2, base + part, axis, full, here[axis], 2 * sign, part
                    )
            for base, sign in SIDES:
                copies[sign, 1] = ag_copy(o, 2, base + 2, axis, full, here[axis], sign)
            waits[o] = begin(copies)
        for part in range(2):
            for o in SEQUENCE:
                axis, full = ORDERS[o][2], ORDERS[o][:2]
                if size[axis] < LONG:
                    continue
                for base, sign in SIDES:
                    waits[o].pop((sign, 2, part)).wait_recv()
                    at = away(axis, -2 * sign)
                    copies = {}
                    if base == 6 * part:
                        copies[sign, 4] = ag_copy(o, 2, base + 5, axis, full, at, 2 * sign, part)
                    copies[sign, 3, part] = ag_copy(o, 2, base + 3 + part, axis, full, at, sign, part)
                    waits[o].update(begin(copies))

        chunk = tokens // size["z"]
        swaps = []
        for place, o in enumerate(LANDING):
            for copy in waits[o].values():
                copy.wait_recv()
            if o == TAGGED:
                spot = (slice(None),) * 4 + (pl.ds(widths[o], TILE),)
                told = to_mate(gathered[o].at[spot], tag_ref.at[turn], 3 + size["z"], turn)
                told.start()
            for z in range(size["z"]):
                rows = pl.ds(z * chunk, chunk)
                x = gathered[o][z].reshape(chunk, gathered[o].shape[-1])[:, : widths[o]]
                total = jnp.dot(
                    x, wgu_ref[starts[o] : starts[o] + widths[o], :], preferred_element_type=F32
                )
                if place:
                    total += gu_ref[rows, :]
                gu_ref[rows, :] = total
                if place == 2:
                    xs_ref[rows, :] = total.astype(BF16)
                    swap = to_mate(xs_ref.at[rows], xr_ref.at[turn, rows], 3 + z, turn)
                    swap.start()
                    swaps.append(swap)
        hidden = wd_ref.shape[0]
        lane = lax.broadcasted_iota(jnp.int32, (tokens, TILE), 1)
        square = (lane >= experts) & (lane < experts + 3)

        def picked(tag, mask):
            return jnp.sum(jnp.where(mask, tag, 0.0), axis=-1, keepdims=True)

        tag = gathered[TAGGED][..., widths[TAGGED] :].reshape(tokens, TILE).astype(F32)
        weight = picked(tag, lane == rack)
        told.wait()
        total = picked(tag, square) + picked(tag_ref[turn].reshape(tokens, TILE).astype(F32), square)
        scale = lax.rsqrt(total / (2 * half) + 1e-6)
        for z in range(size["z"]):
            rows = pl.ds(z * chunk, chunk)
            swaps[z].wait()
            both = gu_ref[rows, :] + xr_ref[turn, rows, :].astype(F32)
            both = both * scale[z * chunk : (z + 1) * chunk]
            gate, up = both[:, :hidden], both[:, hidden:]
            act_ref[rows, :] = (gate / (1.0 + jnp.exp(-gate)) * up).astype(BF16)
        for copy in sends:
            copy.wait_send()

        sends = []
        waits = {}
        for o in SEQUENCE:
            part = jnp.dot(
                act_ref[...], wd_ref[:, starts[o] : starts[o] + widths[o]],
                preferred_element_type=F32,
            )
            partial[o][...] = (part * weight).astype(BF16).reshape(partial[o].shape)
            axis, full = ORDERS[o][2], ORDERS[o][:2]
            if size[axis] < LONG:
                waits[o] = begin({
                    d: rs_copy(
                        o, 0, d - 1, partial[o].at[where_at(full, axis, away(axis, d))],
                        ring_in[o].at[d - 1], axis, d,
                    )
                    for d in range(1, size[axis])
                })
                continue
            copies = {}
            for side, (base, sign) in enumerate(SIDES):
                copies[sign, 4] = rs_copy(
                    o, 0, base + 2, partial[o].at[where_at(full, axis, away(axis, 4 * sign), side)],
                    ring_in[o].at[(side, 1) + inner(full, side)], axis, 2 * sign,
                )
            for half_part in range(2):
                for side, (base, sign) in enumerate(SIDES):
                    p = half_part if side == 0 else 1 - half_part
                    copies[sign, 3, p] = rs_copy(
                        o, 0, base + p,
                        partial[o].at[where_at(full, axis, away(axis, 3 * sign), p)],
                        ring_in[o].at[(side, 0) + inner(full, p)], axis, sign,
                    )
            for side, (base, sign) in enumerate(SIDES):
                copies[sign, 1] = rs_copy(
                    o, 0, base + 3, partial[o].at[where_at(full, axis, away(axis, sign))],
                    ring_in[o].at[side, 2], axis, sign,
                )
            waits[o] = begin(copies)
        for half_part in range(2):
            for o in SEQUENCE:
                axis, full = ORDERS[o][2], ORDERS[o][:2]
                if size[axis] < LONG:
                    continue
                for side, (base, sign) in enumerate(SIDES):
                    p = half_part if side == 0 else 1 - half_part
                    block = inner(full, p)
                    waits[o].pop((sign, 3, p)).wait_recv()
                    total = partial[o][where_at(full, axis, away(axis, 2 * sign), p)].astype(F32)
                    total += ring_in[o][(side, 0) + block].astype(F32)
                    if p == side:
                        waits[o].pop((sign, 4)).wait_recv()
                        total += ring_in[o][(side, 1) + block].astype(F32)
                    ring_out[o][(side,) + block] = total.astype(BF16)
                    waits[o].update(begin({(sign, 2, p): rs_copy(
                        o, 0, base + 4 + p, ring_out[o].at[(side,) + block],
                        ring_in[o].at[(side, 3) + block], axis, 2 * sign,
                    )}))
        flying = {}
        for o in LANDING:
            axis, full = ORDERS[o][2], ORDERS[o][:2]
            for copy in waits[o].values():
                copy.wait_recv()
            total = partial[o][where_at(full, axis, here[axis])].astype(F32)
            if size[axis] < LONG:
                for d in range(1, size[axis]):
                    total += ring_in[o][d - 1].astype(F32)
            else:
                for side in range(2):
                    total += ring_in[o][side, 2].astype(F32) + ring_in[o][side, 3].astype(F32)
            mid_out[o][...] = total.astype(BF16)
            axis = ORDERS[o][1]
            copies = {}
            for d in range(1, size[axis]):
                at = tuple(away(axis, d) if a == axis else pl.ds(0, size[a]) for a in STORED if a in full)
                copies[d] = rs_copy(o, 1, d - 1, mid_out[o].at[at], mid_in[o].at[d - 1], axis, d)
            flying[o] = begin(copies)
        waits = flying
        flying = {}
        for o in LANDING:
            axis, full = ORDERS[o][1], ORDERS[o][:2]
            at = tuple(here[axis] if a == axis else pl.ds(0, size[a]) for a in STORED if a in full)
            total = mid_out[o][at].astype(F32)
            for d in range(1, size[axis]):
                waits[o][d].wait_recv()
                total += mid_in[o][d - 1].astype(F32)
            last_out[o][...] = total.astype(BF16)
            axis = ORDERS[o][0]
            flying[o] = begin({
                d: rs_copy(o, 2, d - 1, last_out[o].at[away(axis, d)], last_in[o].at[d - 1], axis, d)
                for d in range(1, size[axis])
            })
        waits = flying
        for o in LANDING:
            axis = ORDERS[o][0]
            total = last_out[o][here[axis]].astype(F32)
            for d in range(1, size[axis]):
                waits[o][d].wait_recv()
                total += last_in[o][d - 1].astype(F32)
            res_ref[:, starts[o] : starts[o] + widths[o]] += total

            @pl.when(step < steps - 1)
            def _(o=o):
                send_share(o, step + 1)

        for copy in sends:
            copy.wait_send()
        return carry

    lax.fori_loop(0, steps, one_step, 0)

    residual = res_ref[...]
    fs_ref[...] = jnp.where(first_core, residual[1:2], residual[0:1])
    copy = to_mate(fs_ref, fr_ref, 2)
    copy.start()
    kept = jnp.where(first_core, residual[0:1], residual[1:2])
    copy.wait()
    out_ref[:, :half] = jnp.where(first_core, kept, fr_ref[...])
    out_ref[:, half:] = jnp.where(first_core, fr_ref[...], kept)


def per_device(grid, hidden_in, norm_gain, expert_ids, gate_levels, w_gate_up, w_down):
    steps, _, top = expert_ids.shape
    width = hidden_in.shape[1]
    half = width // 2
    hidden = w_down.shape[2]
    tokens = 2 * grid[0] * grid[1] * grid[2]
    widths = tuple(TILE * n for n in shares_of(half // TILE))
    size = dict(zip("xyz", grid))
    stored = tuple(size[a] for a in STORED)

    def dims(names):
        return tuple(size[a] for a in STORED if a in names)

    scratch = [pltpu.VMEM(stored + (2, w + (TILE if o == TAGGED else 0)), BF16) for o, w in enumerate(widths)]
    scratch += [pltpu.VMEM(stored + (2, w), BF16) for w in widths]
    scratch += [
        pltpu.VMEM((tokens, 2 * hidden), F32),
        pltpu.VMEM((tokens, hidden), BF16),
        pltpu.VMEM((tokens, 2 * hidden), BF16),
        pltpu.VMEM((2, tokens, 2 * hidden), BF16),
        pltpu.VMEM((2, half), F32),
        pltpu.VMEM((steps, 2, TILE), F32),
        pltpu.VMEM((steps, TILE), F32),
        pltpu.VMEM((steps, TILE), F32),
        pltpu.VMEM((1, half), F32),
        pltpu.VMEM((1, half), F32),
        pltpu.VMEM((1, half), F32),
        pltpu.VMEM((1, half), F32),
        pltpu.VMEM((2,) + stored + (2, TILE), BF16),
    ]
    lines = [(2, 4) if size[o[2]] >= LONG else (size[o[2]] - 1,) for o in ORDERS]
    scratch += [
        pltpu.VMEM(n + dims(o[:2]) + (2, w), BF16) for n, o, w in zip(lines, ORDERS, widths)
    ]
    scratch += [pltpu.VMEM((2,) + dims(o[:2]) + (2, w), BF16) for o, w in zip(ORDERS, widths)]
    scratch += [pltpu.VMEM(dims(o[:2]) + (2, w), BF16) for o, w in zip(ORDERS, widths)]
    scratch += [
        pltpu.VMEM((size[o[1]] - 1, size[o[0]], 2, w), BF16) for o, w in zip(ORDERS, widths)
    ]
    scratch += [pltpu.VMEM((size[o[0]], 2, w), BF16) for o, w in zip(ORDERS, widths)]
    scratch += [pltpu.VMEM((size[o[0]] - 1, 2, w), BF16) for o, w in zip(ORDERS, widths)]
    most = 12
    scratch += [pltpu.SemaphoreType.DMA((3, 3, most))] * 4
    scratch += [pltpu.SemaphoreType.DMA((2, 4 + size["z"]))] * 2
    return pl.pallas_call(
        functools.partial(kernel, grid, steps, top, widths),
        out_shape=jax.ShapeDtypeStruct((1, width), F32),
        in_specs=[pl.BlockSpec(memory_space=pltpu.VMEM)] * 6,
        out_specs=pl.BlockSpec(memory_space=pltpu.VMEM),
        scratch_shapes=scratch,
        compiler_params=pltpu.CompilerParams(
            collective_id=0, has_side_effects=True, vmem_limit_bytes=48 << 20
        ),
    )(
        hidden_in,
        norm_gain.reshape(1, width),
        expert_ids[:, 0, :],
        gate_levels[:, 0, :],
        w_gate_up[0, 0].reshape(half, 2 * hidden),
        w_down[0, 0],
    )


def solution(mesh, grid=GRID):
    in_specs = (
        P(("rack", "expert"), None),
        P(),
        P(None, ("rack", "expert"), None),
        P(None, ("rack", "expert"), None),
        P("rack", "expert", None, None, None),
        P("rack", "expert", None, None),
    )
    out_specs = P(("rack", "expert"), None)
    return jax.shard_map(
        functools.partial(per_device, grid),
        mesh=mesh, in_specs=in_specs, out_specs=out_specs, check_vma=False,
    )
```
